32 devices in a mesh: dp: 16 (over z, x, core), tensor: 2 (over y).
Axes of the slice: x: 2, y: 2, z: 4, core: 2. Of those that a mesh axis runs over, the one named last changes fastest.
Arguments:
- hidden_in: bfloat16 [8192, 768], P(('dp', 'tensor')), may hold values from -6 to 6
- encoder_states: bfloat16 [8192, 768], P(('dp', 'tensor')), may hold values from -6 to 6
- segments: int32 [16, 512], P('dp'), may hold values from 0 to 3, never falling along the last dimension, each value on 1 to 256 neighbouring positions
- buckets: int32 [512], replicated, may hold values from 0 to 31, as said below
- self_qkv: bfloat16 [1, 768, 3, 768], P(None, 'dp', None, 'tensor'), may hold values from -0.109375 to 0.109375
- self_out: bfloat16 [1, 768, 768], P(None, 'tensor', 'dp'), may hold values from -1.25 to 1.25
- cross_q: bfloat16 [1, 768, 768], P(None, 'dp', 'tensor'), may hold values from -0.109375 to 0.109375
- cross_kv: bfloat16 [1, 768, 2, 768], P(None, 'dp', None, 'tensor'), may hold values from -0.109375 to 0.109375
- cross_out: bfloat16 [1, 768, 768], P(None, 'tensor', 'dp'), may hold values from -1.25 to 1.25
- ffn_in: bfloat16 [1, 768, 2, 2048], P(None, 'dp', None, 'tensor'), may hold values from -0.21875 to 0.21875
- ffn_out: bfloat16 [1, 2048, 768], P(None, 'tensor', 'dp'), may hold values from -0.125 to 0.125
- norm_gains: float32 [1, 3, 768], replicated, may hold values from 0.5 to 1.5
- bias_table: float32 [32, 12], replicated, may hold values from -4 to 4
- cotangent: bfloat16 [8192, 768], P(('dp', 'tensor'))
Outputs:
- output: float32 [8192, 768], P(('dp', 'tensor'))
- grad_hidden: float32 [8192, 768], P(('dp', 'tensor'))
- grad_encoder: float32 [8192, 768], P(('dp', 'tensor'))
- grad_self_qkv: float32 [1, 768, 3, 768], P(None, 'dp', None, 'tensor')
- grad_self_out: float32 [1, 768, 768], P(None, 'tensor', 'dp')
- grad_cross_q: float32 [1, 768, 768], P(None, 'dp', 'tensor')
- grad_cross_kv: float32 [1, 768, 2, 768], P(None, 'dp', None, 'tensor')
- grad_cross_out: float32 [1, 768, 768], P(None, 'tensor', 'dp')
- grad_ffn_in: float32 [1, 768, 2, 2048], P(None, 'dp', None, 'tensor')
- grad_ffn_out: float32 [1, 2048, 768], P(None, 'tensor', 'dp')
- grad_gains: float32 [1, 3, 768], replicated
- grad_table: float32 [32, 12], replicated
The draws below stay inside these ranges and needn't reach their ends.
Inputs may be any that keep to these rules, and one draw needn't show every extreme that they name: `segments`: in each row the document numbers never fall, and no document spans more than 256 positions. buckets[0] is 0, the values never fall and rise by at most 1 from one offset to the next, and the last one is 31.
All inputs are finite; a program needn't handle non-finite values.
Results may differ from the reference program's by a relative error of at most 0.025.
The reference program's roundings to bfloat16 on the way count: a program that leaves them out, or rounds other values in their place, can miss the bound.
Values may be sent and summed in bfloat16 or wider, within the bound.
No kernel may reach another device: no remote copies, remote signals or barrier semaphores. Data moves between devices by JAX's collectives and lax.ppermute only.
A program may use at most 128 MiB of HBM per device.

```python
import math
import jax
import jax.numpy as jnp
import numpy as np
from jax import lax

D = 768
HEADS = 12
DH = 64
FF = 2048
BUCKETS = 32
LENGTH = 512
LAYERS = 1
HD = 768
SEQS = 16
TOKENS = 8192


def draw_buckets(key, part):
    chosen = jax.random.permutation(key, LENGTH - 1)[:BUCKETS - 1] + 1
    flag_rows = jnp.zeros((LENGTH,), jnp.int32).at[chosen].add(1)
    return jnp.cumsum(flag_rows).astype(jnp.int32)


def draw_cotangent(key, part):
    first_key = jax.random.fold_in(key, 11)
    row_index = jnp.arange(TOKENS, dtype=jnp.float32)
    ramp_scale = 1.0 + 2.0 * row_index / TOKENS
    base_draw = jax.random.normal(first_key, (TOKENS, D), jnp.float32)
    return (base_draw * ramp_scale[:, None]).astype(jnp.bfloat16)


def block_levels(stream_key, extent, shards, least, top_value):
    gain, own = 1.0, jax.random.fold_in(stream_key, 6)
    for dim, blocks in shards:
        draws = jnp.exp(jax.random.uniform(jax.random.fold_in(own, dim), (blocks,), jnp.float32, least / len(shards), top_value / len(shards)))
        gain = gain * jnp.repeat(draws, extent[dim] // blocks).reshape([-1 if axis == dim else 1 for axis in range(len(extent))])
    return gain


def profile(number_of, total, limit, skew):
    portions = [(1 << 20) // math.isqrt(standing ** skew) + 1 for standing in range(2, number_of + 1)]
    spare, holding = total - limit - (number_of - 1), [1] * (number_of - 1)
    while spare > 0:
        movable = [i for i in range(number_of - 1) if holding[i] < limit]
        pool, budget = sum([portions[i] for i in movable]), spare
        for i in movable:
            addition = min(limit - holding[i], max(1, budget * portions[i] // pool), spare)
            holding[i] = holding[i] + addition
            spare = spare - addition
    return np.array([limit] + holding)


def uneven_parts(rng, number_of, total, limit, lean):
    if number_of == 2:
        one = jax.random.randint(rng, (), max(1, total - limit), min(limit, total - 1) + 1)
        return jnp.stack([one, total - one])
    sizes = jnp.asarray(profile(number_of, total, limit, lean), jnp.int32)
    pairs = (number_of - 1) // 2
    source_of, receiver = sizes[1:1 + 2 * pairs:2], sizes[2:2 + 2 * pairs:2]
    room = jnp.minimum(source_of - 1, limit - receiver)
    moved = jax.random.randint(jax.random.fold_in(rng, 1), (pairs,), 0, 1 << 20) % (room + 1)
    sizes = sizes.at[1:1 + 2 * pairs:2].set(source_of - moved).at[2:2 + 2 * pairs:2].set(receiver + moved)
    return sizes[jax.random.permutation(jax.random.fold_in(rng, 2), number_of)]


def scatter_about(own_key, extent, spread, reach, pieces=(), kind=jnp.bfloat16):
    loudness = block_levels(own_key, extent, pieces, -0.22, 0.18) if pieces else 1.0
    array = jax.random.normal(own_key, extent, jnp.float32) * spread * loudness
    return jnp.minimum(jnp.maximum(array, -reach), reach).astype(kind)


def setup_inputs(seed: int = 0) -> dict:
    seeds = jax.random.split(jax.random.key(seed), 15)
    return {
        "hidden_in": scatter_about(seeds[0], (TOKENS, D), 1.0, 6.0, ((0, 32),)),
        "encoder_states": scatter_about(seeds[1], (TOKENS, D), 1.0, 6.0, ((0, 32),)),
        "segments": jax.vmap(lambda own: jnp.searchsorted(jnp.cumsum(uneven_parts(own, 4, LENGTH, LENGTH // 2, 0)), jnp.arange(LENGTH), side="right"))(jax.random.split(seeds[2], SEQS)).reshape((SEQS, LENGTH)).astype(jnp.int32),
        "buckets": draw_buckets(jax.random.fold_in(seeds[14], 71), 0),
        "self_qkv": scatter_about(seeds[4], (LAYERS, D, 3, HD), (4 * D) ** -0.5, 0.109375, ((1, 16), (3, 2))),
        "self_out": scatter_about(seeds[5], (LAYERS, HD, D), (HD // 32) ** -0.5, 1.25, ((1, 2), (2, 16))),
        "cross_q": scatter_about(seeds[6], (LAYERS, D, HD), (4 * D) ** -0.5, 0.109375, ((1, 16), (2, 2))),
        "cross_kv": scatter_about(seeds[7], (LAYERS, D, 2, HD), (4 * D) ** -0.5, 0.109375, ((1, 16), (3, 2))),
        "cross_out": scatter_about(seeds[8], (LAYERS, HD, D), (HD // 32) ** -0.5, 1.25, ((1, 2), (2, 16))),
        "ffn_in": scatter_about(seeds[9], (LAYERS, D, 2, FF), D ** -0.5, 0.21875, ((1, 16), (3, 2))),
        "ffn_out": scatter_about(seeds[10], (LAYERS, FF, D), FF ** -0.5, 0.125, ((1, 2), (2, 16))),
        "norm_gains": jnp.clip(1.0 + 0.1 * jax.random.normal(seeds[11], (LAYERS, 3, D), jnp.float32), 0.5, 1.5),
        "bias_table": scatter_about(seeds[12], (BUCKETS, HEADS), 1.0, 4.0, (), jnp.float32),
        "cotangent": draw_cotangent(jax.random.fold_in(seeds[14], 71), 0),
    }


EPSILON = 1e-06
MASKED = -1e+30
HIGHEST = lax.Precision.HIGHEST

@jax.custom_vjp
def low(v):
    return lax.optimization_barrier(v.astype(jnp.bfloat16)).astype(jnp.float32)

@jax.custom_vjp
def low_back(v):
    return v

def low_keep(v):
    return (low(v), None)

def low_pass(kept, grad):
    return (grad,)

def back_keep(v):
    return (v, None)

def back_low(kept, grad):
    return (low(grad),)
low.defvjp(low_keep, low_pass)
low_back.defvjp(back_keep, back_low)

def normed(features, gain_row):
    return features * lax.rsqrt(lax.optimization_barrier(jnp.mean(features * features, axis=-1, keepdims=True)) + EPSILON) * gain_row

def attend(queries, key_rows, value_rows, score_bias, allowed):
    scores = low_back(jnp.einsum('qhd,khd->hqk', queries, key_rows, precision=HIGHEST)) + score_bias
    if allowed is not None:
        scores = jnp.where(allowed[None], scores, MASKED)
    shares = low(jax.nn.softmax(scores, axis=-1))
    return jnp.einsum('hqk,khd->qhd', shares, value_rows, precision=HIGHEST)

def gated(gate_part, up_part):
    return jax.nn.gelu(gate_part, approximate=True) * up_part

def reference(hidden_in, encoder_states, segments, buckets, self_qkv, self_out, cross_q, cross_kv, cross_out, ffn_in, ffn_out, norm_gains, bias_table, cotangent):
    position = jnp.arange(LENGTH, dtype=jnp.int32)
    offsets = jnp.maximum(position[:, None] - position[None, :], 0)
    bucket_map = buckets[offsets]
    causal = position[:, None] >= position[None, :]

    def forward(residual, encoder_rows, w_qkv, w_sout, w_cq, w_ckv, w_cout, w_fin, w_fout, gain_rows, bias_rows):
        rel_bias = jnp.transpose(bias_rows[bucket_map], (2, 0, 1))

        def self_part(inputs):
            queries, key_rows, value_rows, segment_row = inputs
            allowed = causal & (segment_row[:, None] == segment_row[None, :])
            return attend(queries, key_rows, value_rows, rel_bias, allowed)

        def cross_part(inputs):
            queries, key_rows, value_rows = inputs
            return attend(queries, key_rows, value_rows, 0.0, None)
        for layer_index in range(LAYERS):
            normed_self = low(normed(residual, gain_rows[layer_index, 0]))
            projected = low_back(low(jnp.einsum('td,dcf->tcf', normed_self, w_qkv[layer_index], precision=HIGHEST)))
            split_heads = projected.reshape(SEQS, LENGTH, 3, HEADS, DH)
            self_heads = lax.map(jax.checkpoint(self_part), (split_heads[:, :, 0], split_heads[:, :, 1], split_heads[:, :, 2], segments))
            self_mixed = low_back(low(self_heads.reshape(TOKENS, HD)))
            residual = residual + low_back(jnp.dot(self_mixed, w_sout[layer_index], precision=HIGHEST))
            normed_cross = low(normed(residual, gain_rows[layer_index, 1]))
            cross_queries = low_back(low(jnp.dot(normed_cross, w_cq[layer_index], precision=HIGHEST)))
            cross_pairs = low_back(low(jnp.einsum('td,dcf->tcf', encoder_rows, w_ckv[layer_index], precision=HIGHEST)))
            pair_heads = cross_pairs.reshape(SEQS, LENGTH, 2, HEADS, DH)
            cross_heads = lax.map(jax.checkpoint(cross_part), (cross_queries.reshape(SEQS, LENGTH, HEADS, DH), pair_heads[:, :, 0], pair_heads[:, :, 1]))
            cross_mixed = low_back(low(cross_heads.reshape(TOKENS, HD)))
            residual = residual + low_back(jnp.dot(cross_mixed, w_cout[layer_index], precision=HIGHEST))
            normed_ffn = low(normed(residual, gain_rows[layer_index, 2]))
            gate_up = low_back(jnp.einsum('td,dcf->tcf', normed_ffn, w_fin[layer_index], precision=HIGHEST))
            activated = low(gated(gate_up[:, 0], gate_up[:, 1]))
            residual = residual + low_back(jnp.dot(activated, w_fout[layer_index], precision=HIGHEST))
        return residual
    output, backward = jax.vjp(forward, hidden_in.astype(jnp.float32), encoder_states.astype(jnp.float32), self_qkv.astype(jnp.float32), self_out.astype(jnp.float32), cross_q.astype(jnp.float32), cross_kv.astype(jnp.float32), cross_out.astype(jnp.float32), ffn_in.astype(jnp.float32), ffn_out.astype(jnp.float32), norm_gains.astype(jnp.float32), bias_table.astype(jnp.float32))
    gradients = backward(cotangent.astype(jnp.float32))
    return (output, gradients[0], gradients[1], gradients[2], gradients[3], gradients[4], gradients[5], gradients[6], gradients[7], gradients[8], gradients[9], gradients[10])
```

```python
import jax
import jax.numpy as jnp
from jax import lax
from jax.sharding import PartitionSpec as P

DH = 64


EPSILON = 1e-06
MASKED = -1e30


def normed(features, gain_row):
    return (
        features
        * lax.rsqrt(jnp.mean(features * features, axis=-1, keepdims=True) + EPSILON)
        * gain_row
    )


def gated(gate_part, up_part):
    return jax.nn.gelu(gate_part, approximate=True) * up_part


def swap_rows(block):
    return lax.ppermute(block, "tensor", [(0, 1), (1, 0)])


def spread_rows(block):
    if lax.axis_size("tensor") != 2:
        return lax.all_gather(block, "tensor", axis=0, tiled=True)
    other = swap_rows(block)
    first = lax.axis_index("tensor") == 0
    return jnp.concatenate([jnp.where(first, block, other), jnp.where(first, other, block)], axis=0)


def reduce_rows(rows, product):
    if lax.axis_size("tensor") != 2:
        return lax.psum_scatter(product(rows), "tensor", scatter_dimension=0, tiled=True)
    half = rows.shape[0] // 2
    place = lax.axis_index("tensor")
    theirs = lax.dynamic_slice_in_dim(rows, (1 - place) * half, half, 0)
    arrived = swap_rows(product(theirs).astype(jnp.bfloat16))
    kept = product(lax.dynamic_slice_in_dim(rows, place * half, half, 0))
    return kept + arrived.astype(jnp.float32)


def sum_everywhere(block):
    for axis in ("tensor", "dp"):
        size = lax.axis_size(axis)
        if size & (size - 1):
            block = lax.psum(block, axis)
            continue
        step = 1
        while step < size:
            block = block + lax.ppermute(block, axis, [(i, i ^ step) for i in range(size)])
            step *= 2
    return block


def times(rows, weight):
    return jnp.dot(rows, weight, preferred_element_type=jnp.float32)


def times_t(rows, weight):
    return lax.dot_general(
        rows, weight, (((1,), (1,)), ((), ())), preferred_element_type=jnp.float32
    )


def outer(left, right):
    return lax.dot_general(
        left, right, (((0,), (0,)), ((), ())), preferred_element_type=jnp.float32
    ).astype(jnp.bfloat16)


def gather_all(pieces):
    return lax.all_gather(jnp.concatenate(pieces, axis=1), "dp", axis=0, tiled=True)


def scatter_all(pieces):
    joined = jnp.concatenate(pieces, axis=1)
    return lax.psum_scatter(joined, "dp", scatter_dimension=0, tiled=True).astype(jnp.float32)


def head_scores(queries, key_rows, score_bias, allowed):
    scores = (
        jnp.einsum("qhd,khd->hqk", queries, key_rows, preferred_element_type=jnp.float32)
        + score_bias
    )
    if allowed is not None:
        scores = jnp.where(allowed[None], scores, MASKED)
    return scores


def attend(queries, key_rows, value_rows, score_bias, allowed):
    scores = head_scores(queries, key_rows, score_bias, allowed)
    highest = jnp.max(scores, axis=-1, keepdims=True)
    raised = jnp.exp(scores - highest)
    summed = jnp.sum(raised, axis=-1, keepdims=True)
    shares = (raised / summed).astype(jnp.bfloat16)
    mixed_heads = jnp.einsum(
        "hqk,khd->qhd", shares, value_rows, preferred_element_type=jnp.float32
    ).astype(jnp.bfloat16)
    return (mixed_heads, highest + jnp.log(summed))


def attend_back(queries, key_rows, value_rows, score_bias, allowed, log_total, grad_mixed):
    scores = head_scores(queries, key_rows, score_bias, allowed)
    shares = jnp.exp(scores - log_total)
    grad_shares = jnp.einsum(
        "qhd,khd->hqk", grad_mixed, value_rows, preferred_element_type=jnp.float32
    )
    grad_scores = shares * (grad_shares - jnp.sum(shares * grad_shares, axis=-1, keepdims=True))
    rounded = grad_scores.astype(jnp.bfloat16)
    grad_queries = jnp.einsum("hqk,khd->qhd", rounded, key_rows, preferred_element_type=jnp.float32)
    grad_keys = jnp.einsum("hqk,qhd->khd", rounded, queries, preferred_element_type=jnp.float32)
    grad_values = jnp.einsum(
        "hqk,qhd->khd", shares.astype(jnp.bfloat16), grad_mixed, preferred_element_type=jnp.float32
    )
    return (grad_queries, grad_keys, grad_values, grad_scores)


def per_device(
    hidden_in,
    encoder_states,
    segments,
    buckets,
    self_qkv,
    self_out,
    cross_q,
    cross_kv,
    cross_out,
    ffn_in,
    ffn_out,
    norm_gains,
    bias_table,
    cotangent,
):
    seq_count = segments.shape[0]
    length = segments.shape[1]
    group_rows = seq_count * length
    head_width = self_qkv.shape[-1]
    local_heads = head_width // DH
    bucket_count = bias_table.shape[0]
    first_head = lax.axis_index("tensor") * local_heads
    local_table = lax.dynamic_slice_in_dim(bias_table, first_head, local_heads, 1)
    bucket_ids = jnp.arange(bucket_count, dtype=jnp.int32)
    bucket_first = jnp.sum((buckets[:, None] < bucket_ids[None, :]).astype(jnp.int32), axis=0)
    bucket_span = jnp.sum((buckets[:, None] == bucket_ids[None, :]).astype(jnp.int32), axis=0)
    position = jnp.arange(length, dtype=jnp.int32)
    causal = position[:, None] >= position[None, :]
    block_rows = min(length, 128)
    block_count = length // block_rows
    last_block = block_count - 1

    rows = last_block * block_rows + jnp.arange(block_rows, dtype=jnp.int32)
    above = jnp.maximum(rows[:, None] - position[None, :], 0)[:, :, None] - bucket_first
    onehot = ((above >= 0) & (above < bucket_span)).astype(jnp.float32)
    last_rows = jnp.einsum("ijb,bh->hij", onehot, local_table, precision=lax.Precision.HIGHEST)
    rel_bias = jnp.concatenate(
        [
            jnp.pad(
                last_rows[:, :, (last_block - block) * block_rows :],
                ((0, 0), (0, 0), (0, (last_block - block) * block_rows)),
            )
            for block in range(block_count)
        ],
        axis=1,
    )

    def self_forward(inputs):
        queries, key_rows, value_rows, segment_row = inputs
        allowed = causal & (segment_row[:, None] == segment_row[None, :])
        return attend(queries, key_rows, value_rows, rel_bias, allowed)

    def cross_forward(inputs):
        queries, key_rows, value_rows = inputs
        return attend(queries, key_rows, value_rows, 0.0, None)

    def self_backward(accumulated, inputs):
        queries, key_rows, value_rows, segment_row, log_total, grad_mixed = inputs
        allowed = causal & (segment_row[:, None] == segment_row[None, :])
        grad_queries, grad_keys, grad_values, grad_scores = attend_back(
            queries, key_rows, value_rows, rel_bias, allowed, log_total, grad_mixed
        )
        return (accumulated + grad_scores, (grad_queries, grad_keys, grad_values))

    def cross_backward(inputs):
        queries, key_rows, value_rows, log_total, grad_mixed = inputs
        grad_queries, grad_keys, grad_values, unused = attend_back(
            queries, key_rows, value_rows, 0.0, None, log_total, grad_mixed
        )
        return (grad_queries, grad_keys, grad_values)

    width = head_width
    hidden = ffn_in.shape[-1]
    own = self_qkv.shape[1]
    early = gather_all([self_qkv[0].reshape(own, 3 * width), self_out[0].T])
    late = gather_all(
        [
            cross_q[0],
            cross_kv[0].reshape(own, 2 * width),
            cross_out[0].T,
            ffn_in[0].reshape(own, 2 * hidden),
            ffn_out[0].T,
        ]
    )
    w_qkv, w_sout = early[:, : 3 * width], early[:, 3 * width :]
    w_cq = late[:, :width]
    w_ckv = late[:, width : 3 * width]
    w_cout = late[:, 3 * width : 4 * width]
    w_fin = late[:, 4 * width : 4 * width + 2 * hidden]
    w_fout = late[:, 4 * width + 2 * hidden :]

    before_self = hidden_in.astype(jnp.float32)
    normed_self = spread_rows(normed(before_self, norm_gains[0, 0]).astype(jnp.bfloat16))
    encoder_rows = spread_rows(encoder_states)
    grad_out = spread_rows(cotangent)
    projected = times(normed_self, w_qkv).astype(jnp.bfloat16)
    split_heads = projected.reshape(seq_count, length, 3, local_heads, DH)
    self_mixed, self_log = lax.map(
        self_forward, (split_heads[:, :, 0], split_heads[:, :, 1], split_heads[:, :, 2], segments)
    )
    self_flat = self_mixed.reshape(group_rows, width)
    before_cross = before_self + reduce_rows(self_flat, lambda part: times_t(part, w_sout))
    normed_cross = spread_rows(normed(before_cross, norm_gains[0, 1]).astype(jnp.bfloat16))
    cross_queries = times(normed_cross, w_cq).astype(jnp.bfloat16)
    cross_pairs = times(encoder_rows, w_ckv).astype(jnp.bfloat16)
    pair_heads = cross_pairs.reshape(seq_count, length, 2, local_heads, DH)
    query_heads = cross_queries.reshape(seq_count, length, local_heads, DH)
    cross_mixed, cross_log = lax.map(
        cross_forward, (query_heads, pair_heads[:, :, 0], pair_heads[:, :, 1])
    )
    cross_flat = cross_mixed.reshape(group_rows, width)
    before_ffn = before_cross + reduce_rows(cross_flat, lambda part: times_t(part, w_cout))
    normed_ffn = spread_rows(normed(before_ffn, norm_gains[0, 2]).astype(jnp.bfloat16))
    gate_up = times(normed_ffn, w_fin)
    gate, up = gate_up[:, :hidden], gate_up[:, hidden:]
    activated = gated(gate, up).astype(jnp.bfloat16)
    residual = before_ffn + reduce_rows(activated, lambda part: times_t(part, w_fout))

    grad_rows = cotangent.astype(jnp.float32)
    grad_act = times(grad_out, w_fout)
    unused_value, gate_back = jax.vjp(gated, gate, up)
    grad_gate, grad_up = gate_back(grad_act)
    grad_pair = jnp.concatenate([grad_gate, grad_up], axis=1).astype(jnp.bfloat16)
    grad_normed = reduce_rows(grad_pair, lambda part: times_t(part, w_fin))
    ffn_sums = scatter_all([outer(normed_ffn, grad_pair), outer(grad_out, activated)])
    unused_value, norm_back = jax.vjp(normed, before_ffn, norm_gains[0, 2])
    grad_prev, gain_ffn = norm_back(grad_normed)
    grad_rows = grad_rows + grad_prev

    grad_out = spread_rows(grad_rows.astype(jnp.bfloat16))
    grad_cmix = times(grad_out, w_cout).astype(jnp.bfloat16)
    grad_wcout = outer(grad_out, cross_flat)
    grad_cq, grad_ck, grad_cv = lax.map(
        cross_backward,
        (
            query_heads,
            pair_heads[:, :, 0],
            pair_heads[:, :, 1],
            cross_log,
            grad_cmix.reshape(seq_count, length, local_heads, DH),
        ),
    )
    grad_cq_rows = grad_cq.reshape(group_rows, width).astype(jnp.bfloat16)
    grad_ckv_rows = jnp.concatenate(
        [
            grad_ck.reshape(group_rows, width).astype(jnp.bfloat16),
            grad_cv.reshape(group_rows, width).astype(jnp.bfloat16),
        ],
        axis=1,
    )
    grad_normed = reduce_rows(grad_cq_rows, lambda part: times_t(part, w_cq))
    grad_encoder = reduce_rows(grad_ckv_rows, lambda part: times_t(part, w_ckv))
    grad_wcq = outer(normed_cross, grad_cq_rows)
    grad_wckv = outer(encoder_rows, grad_ckv_rows)
    unused_value, norm_back = jax.vjp(normed, before_cross, norm_gains[0, 1])
    grad_prev, gain_cross = norm_back(grad_normed)
    grad_rows = grad_rows + grad_prev

    grad_out = spread_rows(grad_rows.astype(jnp.bfloat16))
    grad_smix = times(grad_out, w_sout).astype(jnp.bfloat16)
    grad_wsout = outer(grad_out, self_flat)
    grad_bias, self_grads = lax.scan(
        self_backward,
        jnp.zeros_like(rel_bias),
        (
            split_heads[:, :, 0],
            split_heads[:, :, 1],
            split_heads[:, :, 2],
            segments,
            self_log,
            grad_smix.reshape(seq_count, length, local_heads, DH),
        ),
    )
    grad_proj = jnp.concatenate(
        [part.reshape(group_rows, width).astype(jnp.bfloat16) for part in self_grads], axis=1
    )
    grad_wqkv = outer(normed_self, grad_proj)
    rest_sums = scatter_all([grad_wqkv, grad_wsout, grad_wcq, grad_wckv, grad_wcout])
    grad_normed = reduce_rows(grad_proj, lambda part: times_t(part, w_qkv))
    unused_value, norm_back = jax.vjp(normed, before_self, norm_gains[0, 0])
    grad_prev, gain_self = norm_back(grad_normed)
    grad_rows = grad_rows + grad_prev

    folded = sum(
        jnp.pad(
            grad_bias[
                :, block * block_rows : (block + 1) * block_rows, : (block + 1) * block_rows
            ],
            ((0, 0), (0, 0), ((last_block - block) * block_rows, 0)),
        )
        for block in range(block_count)
    )
    grad_local = jnp.einsum("hij,ijb->hb", folded, onehot, precision=lax.Precision.HIGHEST)
    features = before_self.shape[1]
    grad_table = lax.dynamic_update_slice(
        jnp.zeros((bias_table.shape[1], features), jnp.float32),
        grad_local,
        (first_head, jnp.int32(0)),
    )
    small = jnp.concatenate([jnp.stack([gain_self, gain_cross, gain_ffn]), grad_table], axis=0)
    small = sum_everywhere(small)
    edge = 3 * width
    return (
        residual,
        grad_rows,
        grad_encoder,
        rest_sums[:, :edge].reshape(1, own, 3, width),
        rest_sums[:, edge : edge + width].T[None],
        rest_sums[:, edge + width : edge + 2 * width][None],
        rest_sums[:, edge + 2 * width : edge + 4 * width].reshape(1, own, 2, width),
        rest_sums[:, edge + 4 * width :].T[None],
        ffn_sums[:, : 2 * hidden].reshape(1, own, 2, hidden),
        ffn_sums[:, 2 * hidden :].T[None],
        small[None, :3],
        small[3:, :bucket_count].T,
    )


def solution(mesh):
    in_specs = (
        P(("dp", "tensor"), None),
        P(("dp", "tensor"), None),
        P("dp", None),
        P(),
        P(None, "dp", None, "tensor"),
        P(None, "tensor", "dp"),
        P(None, "dp", "tensor"),
        P(None, "dp", None, "tensor"),
        P(None, "tensor", "dp"),
        P(None, "dp", None, "tensor"),
        P(None, "tensor", "dp"),
        P(),
        P(),
        P(("dp", "tensor"), None),
    )
    out_specs = (
        P(("dp", "tensor"), None),
        P(("dp", "tensor"), None),
        P(("dp", "tensor"), None),
        P(None, "dp", None, "tensor"),
        P(None, "tensor", "dp"),
        P(None, "dp", "tensor"),
        P(None, "dp", None, "tensor"),
        P(None, "tensor", "dp"),
        P(None, "dp", None, "tensor"),
        P(None, "tensor", "dp"),
        P(),
        P(),
    )
    return jax.shard_map(
        per_device, mesh=mesh, in_specs=in_specs, out_specs=out_specs, check_vma=False
    )
```

```python
import jax
import jax.numpy as jnp
from jax import lax
from jax.sharding import PartitionSpec as P

DH = 64


EPSILON = 1e-06
MASKED = -1e30


def normed(features, gain_row):
    return (
        features
        * lax.rsqrt(jnp.mean(features * features, axis=-1, keepdims=True) + EPSILON)
        * gain_row
    )


def gated(gate_part, up_part):
    return jax.nn.gelu(gate_part, approximate=True) * up_part


def swap_rows(block):
    return lax.ppermute(block, "tensor", [(0, 1), (1, 0)])


def spread_rows(block):
    if lax.axis_size("tensor") != 2:
        return lax.all_gather(block, "tensor", axis=0, tiled=True)
    other = swap_rows(block)
    first = lax.axis_index("tensor") == 0
    return jnp.concatenate([jnp.where(first, block, other), jnp.where(first, other, block)], axis=0)


def reduce_rows(rows, product):
    if lax.axis_size("tensor") != 2:
        return lax.psum_scatter(product(rows), "tensor", scatter_dimension=0, tiled=True)
    half = rows.shape[0] // 2
    place = lax.axis_index("tensor")
    theirs = lax.dynamic_slice_in_dim(rows, (1 - place) * half, half, 0)
    arrived = swap_rows(product(theirs).astype(jnp.bfloat16))
    kept = product(lax.dynamic_slice_in_dim(rows, place * half, half, 0))
    return kept + arrived.astype(jnp.float32)


def sum_everywhere(block):
    for axis in ("tensor", "dp"):
        size = lax.axis_size(axis)
        if size & (size - 1):
            block = lax.psum(block, axis)
            continue
        step = 1
        while step < size:
            block = block + lax.ppermute(block, axis, [(i, i ^ step) for i in range(size)])
            step *= 2
    return block


def times(rows, weight):
    return jnp.dot(rows, weight, preferred_element_type=jnp.float32)


def times_t(rows, weight):
    return lax.dot_general(
        rows, weight, (((1,), (1,)), ((), ())), preferred_element_type=jnp.float32
    )


def outer(left, right):
    return lax.dot_general(
        left, right, (((0,), (0,)), ((), ())), preferred_element_type=jnp.float32
    )


def gather_all(pieces):
    return lax.all_gather(jnp.concatenate(pieces, axis=1), "dp", axis=0, tiled=True)


def scatter_all(pieces):
    joined = jnp.concatenate([piece.astype(jnp.bfloat16) for piece in pieces], axis=1)
    return lax.psum_scatter(joined, "dp", scatter_dimension=0, tiled=True).astype(jnp.float32)


def scatter_halves(pieces):
    size = lax.axis_size("dp")
    if size & (size - 1):
        return scatter_all(pieces)
    block = jnp.concatenate(pieces, axis=1)
    own, lanes = block.shape[0] // size, block.shape[1]
    place = lax.axis_index("dp")
    step = 1
    while step < size:
        groups = block.reshape(size // (2 * step), 2, own, lanes)
        bit = (place // step) % 2
        sent = lax.dynamic_index_in_dim(groups, 1 - bit, 1, keepdims=False).astype(jnp.bfloat16)
        kept = lax.dynamic_index_in_dim(groups, bit, 1, keepdims=False)
        arrived = lax.ppermute(sent, "dp", [(i, i ^ step) for i in range(size)])
        block = kept + arrived.astype(jnp.float32)
        step *= 2
    return block.reshape(own, lanes)


def head_scores(queries, key_rows, score_bias, allowed):
    scores = (
        jnp.einsum("qhd,khd->hqk", queries, key_rows, preferred_element_type=jnp.float32)
        + score_bias
    )
    if allowed is not None:
        scores = jnp.where(allowed[None], scores, MASKED)
    return scores


def attend(queries, key_rows, value_rows, score_bias, allowed):
    scores = head_scores(queries, key_rows, score_bias, allowed)
    highest = jnp.max(scores, axis=-1, keepdims=True)
    raised = jnp.exp(scores - highest)
    summed = jnp.sum(raised, axis=-1, keepdims=True)
    shares = (raised / summed).astype(jnp.bfloat16)
    mixed_heads = jnp.einsum(
        "hqk,khd->qhd", shares, value_rows, preferred_element_type=jnp.float32
    ).astype(jnp.bfloat16)
    return (mixed_heads, highest + jnp.log(summed))


def attend_back(queries, key_rows, value_rows, score_bias, allowed, log_total, grad_mixed):
    scores = head_scores(queries, key_rows, score_bias, allowed)
    shares = jnp.exp(scores - log_total)
    grad_shares = jnp.einsum(
        "qhd,khd->hqk", grad_mixed, value_rows, preferred_element_type=jnp.float32
    )
    grad_scores = shares * (grad_shares - jnp.sum(shares * grad_shares, axis=-1, keepdims=True))
    rounded = grad_scores.astype(jnp.bfloat16)
    grad_queries = jnp.einsum("hqk,khd->qhd", rounded, key_rows, preferred_element_type=jnp.float32)
    grad_keys = jnp.einsum("hqk,qhd->khd", rounded, queries, preferred_element_type=jnp.float32)
    grad_values = jnp.einsum(
        "hqk,qhd->khd", shares.astype(jnp.bfloat16), grad_mixed, preferred_element_type=jnp.float32
    )
    return (grad_queries, grad_keys, grad_values, grad_scores)


def per_device(
    hidden_in,
    encoder_states,
    segments,
    buckets,
    self_qkv,
    self_out,
    cross_q,
    cross_kv,
    cross_out,
    ffn_in,
    ffn_out,
    norm_gains,
    bias_table,
    cotangent,
):
    seq_count = segments.shape[0]
    length = segments.shape[1]
    group_rows = seq_count * length
    head_width = self_qkv.shape[-1]
    local_heads = head_width // DH
    bucket_count = bias_table.shape[0]
    first_head = lax.axis_index("tensor") * local_heads
    local_table = lax.dynamic_slice_in_dim(bias_table, first_head, local_heads, 1)
    bucket_ids = jnp.arange(bucket_count, dtype=jnp.int32)
    bucket_first = jnp.sum((buckets[:, None] < bucket_ids[None, :]).astype(jnp.int32), axis=0)
    bucket_span = jnp.sum((buckets[:, None] == bucket_ids[None, :]).astype(jnp.int32), axis=0)
    position = jnp.arange(length, dtype=jnp.int32)
    causal = position[:, None] >= position[None, :]
    block_rows = min(length, 128)
    block_count = length // block_rows
    last_block = block_count - 1

    rows = last_block * block_rows + jnp.arange(block_rows, dtype=jnp.int32)
    above = jnp.maximum(rows[:, None] - position[None, :], 0)[:, :, None] - bucket_first
    onehot = ((above >= 0) & (above < bucket_span)).astype(jnp.float32)
    last_rows = jnp.einsum("ijb,bh->hij", onehot, local_table, precision=lax.Precision.HIGHEST)
    rel_bias = jnp.concatenate(
        [
            jnp.pad(
                last_rows[:, :, (last_block - block) * block_rows :],
                ((0, 0), (0, 0), (0, (last_block - block) * block_rows)),
            )
            for block in range(block_count)
        ],
        axis=1,
    )

    def self_forward(inputs):
        queries, key_rows, value_rows, segment_row = inputs
        allowed = causal & (segment_row[:, None] == segment_row[None, :])
        return attend(queries, key_rows, value_rows, rel_bias, allowed)

    def cross_forward(inputs):
        queries, key_rows, value_rows = inputs
        return attend(queries, key_rows, value_rows, 0.0, None)

    def self_backward(accumulated, inputs):
        queries, key_rows, value_rows, segment_row, log_total, grad_mixed = inputs
        allowed = causal & (segment_row[:, None] == segment_row[None, :])
        grad_queries, grad_keys, grad_values, grad_scores = attend_back(
            queries, key_rows, value_rows, rel_bias, allowed, log_total, grad_mixed
        )
        return (accumulated + grad_scores, (grad_queries, grad_keys, grad_values))

    def cross_backward(inputs):
        queries, key_rows, value_rows, log_total, grad_mixed = inputs
        grad_queries, grad_keys, grad_values, unused = attend_back(
            queries, key_rows, value_rows, 0.0, None, log_total, grad_mixed
        )
        return (grad_queries, grad_keys, grad_values)

    width = head_width
    hidden = ffn_in.shape[-1]
    own = self_qkv.shape[1]
    early = gather_all([self_qkv[0].reshape(own, 3 * width), self_out[0].T])
    late = gather_all(
        [
            cross_q[0],
            cross_kv[0].reshape(own, 2 * width),
            cross_out[0].T,
            ffn_in[0].reshape(own, 2 * hidden),
            ffn_out[0].T,
        ]
    )
    w_qkv, w_sout = early[:, : 3 * width], early[:, 3 * width :]
    w_cq = late[:, :width]
    w_ckv = late[:, width : 3 * width]
    w_cout = late[:, 3 * width : 4 * width]
    w_fin = late[:, 4 * width : 4 * width + 2 * hidden]
    w_fout = late[:, 4 * width + 2 * hidden :]

    before_self = hidden_in.astype(jnp.float32)
    normed_self = spread_rows(normed(before_self, norm_gains[0, 0]).astype(jnp.bfloat16))
    encoder_rows = spread_rows(encoder_states)
    grad_out = spread_rows(cotangent)
    normed_self, encoder_rows, grad_out = lax.optimization_barrier(
        (normed_self, encoder_rows, grad_out)
    )
    projected = times(normed_self, w_qkv).astype(jnp.bfloat16)
    split_heads = projected.reshape(seq_count, length, 3, local_heads, DH)
    self_mixed, self_log = lax.map(
        self_forward, (split_heads[:, :, 0], split_heads[:, :, 1], split_heads[:, :, 2], segments)
    )
    self_flat = self_mixed.reshape(group_rows, width)
    before_cross = before_self + reduce_rows(self_flat, lambda part: times_t(part, w_sout))
    normed_cross = spread_rows(normed(before_cross, norm_gains[0, 1]).astype(jnp.bfloat16))
    cross_queries = times(normed_cross, w_cq).astype(jnp.bfloat16)
    cross_pairs = times(encoder_rows, w_ckv).astype(jnp.bfloat16)
    pair_heads = cross_pairs.reshape(seq_count, length, 2, local_heads, DH)
    query_heads = cross_queries.reshape(seq_count, length, local_heads, DH)
    cross_mixed, cross_log = lax.map(
        cross_forward, (query_heads, pair_heads[:, :, 0], pair_heads[:, :, 1])
    )
    cross_flat = cross_mixed.reshape(group_rows, width)
    before_ffn = before_cross + reduce_rows(cross_flat, lambda part: times_t(part, w_cout))
    normed_ffn = spread_rows(normed(before_ffn, norm_gains[0, 2]).astype(jnp.bfloat16))
    gate_up = times(normed_ffn, w_fin)
    gate, up = gate_up[:, :hidden], gate_up[:, hidden:]
    activated = gated(gate, up).astype(jnp.bfloat16)
    residual = before_ffn + reduce_rows(activated, lambda part: times_t(part, w_fout))

    grad_rows = cotangent.astype(jnp.float32)
    grad_act = lax.optimization_barrier(times(grad_out, w_fout))
    unused_value, gate_back = jax.vjp(gated, gate, up)
    grad_gate, grad_up = gate_back(grad_act)
    grad_pair = jnp.concatenate([grad_gate, grad_up], axis=1).astype(jnp.bfloat16)
    grad_normed = reduce_rows(grad_pair, lambda part: times_t(part, w_fin))
    ffn_sums = scatter_all([outer(normed_ffn, grad_pair), outer(grad_out, activated)])
    unused_value, norm_back = jax.vjp(normed, before_ffn, norm_gains[0, 2])
    grad_prev, gain_ffn = norm_back(grad_normed)
    grad_rows = grad_rows + grad_prev

    grad_out = spread_rows(grad_rows.astype(jnp.bfloat16))
    grad_cmix = times(grad_out, w_cout).astype(jnp.bfloat16)
    grad_wcout = outer(grad_out, cross_flat)
    grad_cq, grad_ck, grad_cv = lax.map(
        cross_backward,
        (
            query_heads,
            pair_heads[:, :, 0],
            pair_heads[:, :, 1],
            cross_log,
            grad_cmix.reshape(seq_count, length, local_heads, DH),
        ),
    )
    grad_cq_rows = grad_cq.reshape(group_rows, width).astype(jnp.bfloat16)
    grad_ckv_rows = jnp.concatenate(
        [
            grad_ck.reshape(group_rows, width).astype(jnp.bfloat16),
            grad_cv.reshape(group_rows, width).astype(jnp.bfloat16),
        ],
        axis=1,
    )
    grad_normed = reduce_rows(grad_cq_rows, lambda part: times_t(part, w_cq))
    grad_encoder = reduce_rows(grad_ckv_rows, lambda part: times_t(part, w_ckv))
    grad_wcq = outer(normed_cross, grad_cq_rows)
    grad_wckv = outer(encoder_rows, grad_ckv_rows)
    cross_sums = scatter_halves([grad_wcq, grad_wckv, grad_wcout])
    unused_value, norm_back = jax.vjp(normed, before_cross, norm_gains[0, 1])
    grad_prev, gain_cross = norm_back(grad_normed)
    grad_rows = grad_rows + grad_prev

    grad_out = spread_rows(grad_rows.astype(jnp.bfloat16))
    grad_smix = times(grad_out, w_sout).astype(jnp.bfloat16)
    grad_wsout = outer(grad_out, self_flat)
    grad_bias, self_grads = lax.scan(
        self_backward,
        jnp.zeros_like(rel_bias),
        (
            split_heads[:, :, 0],
            split_heads[:, :, 1],
            split_heads[:, :, 2],
            segments,
            self_log,
            grad_smix.reshape(seq_count, length, local_heads, DH),
        ),
    )
    grad_proj = jnp.concatenate(
        [part.reshape(group_rows, width).astype(jnp.bfloat16) for part in self_grads], axis=1
    )
    grad_wqkv = outer(normed_self, grad_proj)
    self_sums = scatter_halves([grad_wqkv, grad_wsout])
    grad_normed = reduce_rows(grad_proj, lambda part: times_t(part, w_qkv))
    unused_value, norm_back = jax.vjp(normed, before_self, norm_gains[0, 0])
    grad_prev, gain_self = norm_back(grad_normed)
    grad_rows = grad_rows + grad_prev

    folded = sum(
        jnp.pad(
            grad_bias[
                :, block * block_rows : (block + 1) * block_rows, : (block + 1) * block_rows
            ],
            ((0, 0), (0, 0), ((last_block - block) * block_rows, 0)),
        )
        for block in range(block_count)
    )
    grad_local = jnp.einsum("hij,ijb->hb", folded, onehot, precision=lax.Precision.HIGHEST)
    features = before_self.shape[1]
    grad_table = lax.dynamic_update_slice(
        jnp.zeros((bias_table.shape[1], features), jnp.float32),
        grad_local,
        (first_head, jnp.int32(0)),
    )
    small = jnp.concatenate([jnp.stack([gain_self, gain_cross, gain_ffn]), grad_table], axis=0)
    small = sum_everywhere(small)
    edge = 3 * width
    return (
        residual,
        grad_rows,
        grad_encoder,
        self_sums[:, :edge].reshape(1, own, 3, width),
        self_sums[:, edge:].T[None],
        cross_sums[:, :width][None],
        cross_sums[:, width:edge].reshape(1, own, 2, width),
        cross_sums[:, edge:].T[None],
        ffn_sums[:, : 2 * hidden].reshape(1, own, 2, hidden),
        ffn_sums[:, 2 * hidden :].T[None],
        small[None, :3],
        small[3:, :bucket_count].T,
    )


def solution(mesh):
    in_specs = (
        P(("dp", "tensor"), None),
        P(("dp", "tensor"), None),
        P("dp", None),
        P(),
        P(None, "dp", None, "tensor"),
        P(None, "tensor", "dp"),
        P(None, "dp", "tensor"),
        P(None, "dp", None, "tensor"),
        P(None, "tensor", "dp"),
        P(None, "dp", None, "tensor"),
        P(None, "tensor", "dp"),
        P(),
        P(),
        P(("dp", "tensor"), None),
    )
    out_specs = (
        P(("dp", "tensor"), None),
        P(("dp", "tensor"), None),
        P(("dp", "tensor"), None),
        P(None, "dp", None, "tensor"),
        P(None, "tensor", "dp"),
        P(None, "dp", "tensor"),
        P(None, "dp", None, "tensor"),
        P(None, "tensor", "dp"),
        P(None, "dp", None, "tensor"),
        P(None, "tensor", "dp"),
        P(),
        P(),
    )
    return jax.shard_map(
        per_device, mesh=mesh, in_specs=in_specs, out_specs=out_specs, check_vma=False
    )
```
